32 devices in a mesh: parts: 2 (over y), gz: 4 (over x, core), ty: 4 (over z).
Axes of the slice: x: 2, y: 2, z: 4, core: 2. Of those that a mesh axis runs over, the one named last changes fastest.
Arguments:
- sections: bfloat16 [8, 1024, 2048], P(('parts', 'gz'), 'ty'), parts along dimension 0, may hold values from -6 to 6
- boundary: bfloat16 [2048, 2048], P(('parts', 'ty')), parts along dimension 0, may hold values from -5 to 5
- row_shift: int32 [8, 1024], P(('parts', 'gz'), 'ty'), parts along dimension 0, may hold values from -64 to 63
- row_frac: int32 [8, 1024], P(('parts', 'gz'), 'ty'), parts along dimension 0, may hold values from 0 to 255
- col_shift: int32 [8, 2048], P(('parts', 'gz')), parts along dimension 0, may hold values from -64 to 63
- col_frac: int32 [8, 2048], P(('parts', 'gz')), parts along dimension 0, may hold values from 0 to 255
- peak_shift: int32 [2, 8, 8, 16], P(None, ('parts', 'gz'), 'ty'), parts along dimension 1, may hold values from -8 to 8
Outputs:
- rendered: bfloat16 [8, 1024, 2048], P(('parts', 'gz'), 'ty'), parts along dimension 0
- flow: float32 [2, 8, 8, 16], P(None, ('parts', 'gz'), 'ty'), parts along dimension 1
The draws below stay inside these ranges and needn't reach their ends.
There are 2 independent parts, one for each index of `parts`. The reference program is written for one: setup_inputs(seed, part) draws one part's arguments, and reference() takes and returns one part's arrays. A program takes and returns all parts, laid end to end along the dimension named above; each array names one. Nothing has to cross between parts.
All inputs are finite; a program needn't handle non-finite values.
Results may differ from the reference program's by a relative error of at most 0.0049.
Values may be sent and summed in bfloat16 or wider, within the bound.
A program may use at most 64 MiB of HBM per device.

```python
import jax
import jax.numpy as jnp
from jax import lax

PATCH = 128
NX = 2048
MARGIN = 64
COL_REACH = 64
MAX_PEAK = 8
SMOOTH_PASSES = 2
NZ = 4
NY = 1024
PY = 8
PX = 16


def set_ends(entries, own_key, least, high):
    shape = entries.shape
    place = [jax.random.randint(jax.random.fold_in(own_key, axis), (), 0, shape[axis]) for axis in range(len(shape))]
    entries = entries.at[tuple(place)].set(least)
    longest = shape.index(max(shape))
    place[longest] = (place[longest] + 1) % shape[longest]
    return entries.at[tuple(place)].set(high)


def shard_levels(rng, dims, split, smallest, high):
    gain = 1.0
    for position, blocks in split:
        heights = jax.random.uniform(jax.random.fold_in(jax.random.fold_in(rng, 6), position), (blocks,), jnp.float32, smallest / len(split), high / len(split))
        gain = gain * jnp.repeat(jnp.exp(heights), dims[position] // blocks).reshape((-1,) + (1,) * (len(dims) - 1 - position))
    return gain


def noise(stream_key, extent, deviation, reach, pieces=(), kind=jnp.bfloat16):
    values = jax.random.normal(stream_key, extent, jnp.float32) * deviation
    if len(pieces) > 0:
        values = shard_levels(stream_key, extent, pieces, -0.22, 0.18) * values
    return jnp.clip(values, min=-reach, max=reach).astype(kind)


def setup_inputs(seed: int = 0, part: int = 0) -> dict:
    seeds = jax.random.split(jax.random.key(seed), 8)
    own_keys = jax.random.split(jax.random.fold_in(seeds[7], part), 8)
    return {
        "sections": noise(own_keys[0], (NZ, NY, NX), 1.0, 6.0, ((0, 4), (1, 4))),
        "boundary": noise(own_keys[1], (NY, NX), 0.7, 5.0, ((0, 4),)),
        "row_shift": set_ends(jax.random.randint(own_keys[2], (NZ, NY), -MARGIN, MARGIN), jax.random.fold_in(own_keys[2], 1), -MARGIN, MARGIN - 1).astype(jnp.int32),
        "row_frac": set_ends(jax.random.randint(own_keys[3], (NZ, NY), 0, 256), jax.random.fold_in(own_keys[3], 1), 0, 255).astype(jnp.int32),
        "col_shift": set_ends(jax.random.randint(own_keys[4], (NZ, NX), -COL_REACH, COL_REACH), jax.random.fold_in(own_keys[4], 1), -COL_REACH, COL_REACH - 1).astype(jnp.int32),
        "col_frac": set_ends(jax.random.randint(own_keys[5], (NZ, NX), 0, 256), jax.random.fold_in(own_keys[5], 1), 0, 255).astype(jnp.int32),
        "peak_shift": set_ends(jax.random.randint(own_keys[6], (2, NZ, PY, PX), -MAX_PEAK, MAX_PEAK + 1), jax.random.fold_in(own_keys[6], 1), -MAX_PEAK, MAX_PEAK).astype(jnp.int32),
    }


blur_taps = (0.0625, 0.25, 0.375, 0.25, 0.0625)


def render_section(section, shift_rows, frac_rows, shift_cols, frac_cols):
    sec_height = section.shape[0]
    sec_width = section.shape[1]
    row_ids = jnp.arange(sec_height, dtype=jnp.int32)
    source_row = jnp.clip(row_ids + shift_rows, 0, sec_height - 2).astype(jnp.int32)
    row_weight = (frac_rows.astype(jnp.float32) / 256.0)[:, None]
    upper_rows = jnp.take(section, source_row, axis=0).astype(jnp.float32)
    lower_rows = jnp.take(section, source_row + 1, axis=0).astype(jnp.float32)
    row_mix = ((1.0 - row_weight) * upper_rows + row_weight * lower_rows).astype(jnp.bfloat16)
    col_ids = jnp.arange(sec_width, dtype=jnp.int32)
    source_col = jnp.clip(col_ids + shift_cols, 0, sec_width - 2).astype(jnp.int32)
    col_weight = (frac_cols.astype(jnp.float32) / 256.0)[None, :]
    first_cols = jnp.take(row_mix, source_col, axis=1).astype(jnp.float32)
    second_cols = jnp.take(row_mix, source_col + 1, axis=1).astype(jnp.float32)
    return ((1.0 - col_weight) * first_cols + col_weight * second_cols).astype(jnp.bfloat16)


def to_patches(section):
    return section.reshape(PY, PATCH, PX, PATCH).transpose(0, 2, 1, 3).astype(jnp.float32)


def window_of(current, earlier, peak_row, peak_col):
    cur_patches = to_patches(current)
    old_patches = to_patches(earlier)
    spectrum = jnp.conj(jnp.fft.fft2(cur_patches)) * jnp.fft.fft2(old_patches)
    correlation = jnp.real(jnp.fft.ifft2(spectrum)) / PATCH
    offsets = jnp.arange(3, dtype=jnp.int32) - 1
    patch_ids = jnp.arange(PATCH, dtype=jnp.int32)
    select_row = (((peak_row[..., None] + offsets) % PATCH)[..., None] == patch_ids).astype(correlation.dtype)
    select_col = (((peak_col[..., None] + offsets) % PATCH)[..., None] == patch_ids).astype(correlation.dtype)
    return jnp.einsum("abip,abpq,abjq->abij", select_row, correlation, select_col, precision=lax.Precision.HIGHEST)


def centroid_flow(window, peak_row, peak_col):
    offsets = jnp.arange(3, dtype=jnp.int32).astype(jnp.float32) - 1.0
    weights = jnp.maximum(window, 0.0)
    weight_sum = jnp.maximum(jnp.sum(weights, axis=(-2, -1)), 1.0)
    flow_row = peak_row.astype(jnp.float32) + jnp.sum(weights * offsets[:, None], axis=(-2, -1)) / weight_sum
    flow_col = peak_col.astype(jnp.float32) + jnp.sum(weights * offsets[None, :], axis=(-2, -1)) / weight_sum
    return flow_row, flow_col


def blur_rows(padded, n_rows):
    result = blur_taps[0] * padded[..., 0:n_rows, :]
    for offset in range(1, 5):
        result = result + blur_taps[offset] * padded[..., offset:offset + n_rows, :]
    return result


def blur_cols(grid_values):
    n_cols = grid_values.shape[-1]
    padded = jnp.pad(grid_values, [(0, 0)] * (grid_values.ndim - 1) + [(2, 2)])
    result = blur_taps[0] * padded[..., 0:n_cols]
    for offset in range(1, 5):
        result = result + blur_taps[offset] * padded[..., offset:offset + n_cols]
    return result


def reference(sections, boundary, row_shift, row_frac, col_shift, col_frac, peak_shift):
    rendered = jnp.stack([render_section(sections[section_id], row_shift[section_id], row_frac[section_id], col_shift[section_id], col_frac[section_id]) for section_id in range(NZ)])
    previous = jnp.concatenate([boundary[None], rendered[:-1]], axis=0)
    rows_out = []
    cols_out = []
    for section_id in range(NZ):
        window = window_of(rendered[section_id], previous[section_id], peak_shift[0, section_id], peak_shift[1, section_id])
        flow_row, flow_col = centroid_flow(window, peak_shift[0, section_id], peak_shift[1, section_id])
        rows_out.append(flow_row)
        cols_out.append(flow_col)
    flow_now = jnp.stack([jnp.stack(rows_out), jnp.stack(cols_out)])
    unit_field = jnp.ones_like(flow_now[0:1])
    padding = [(0, 0), (0, 0), (2, 2), (0, 0)]
    for repeat in range(SMOOTH_PASSES):
        stacked = jnp.concatenate([flow_now, unit_field], axis=0)
        blurred = blur_cols(blur_rows(jnp.pad(stacked, padding), PY))
        flow_now = blurred[0:2] / blurred[2:3]
    return rendered, flow_now
```

```python
import functools

import jax
import jax.numpy as jnp
import numpy as np
from jax import lax
from jax.experimental import pallas as pl
from jax.experimental.pallas import tpu as pltpu
from jax.sharding import PartitionSpec as P

PATCH = 128
MARGIN = 64
SMOOTH_PASSES = 2
TAPS = (0.0625, 0.25, 0.375, 0.25, 0.0625)
BLOCK = 256


def smooth_operator(n):
    kernel = np.zeros((n, n))
    for k, tap in enumerate(TAPS):
        kernel += tap * np.eye(n, k=k - 2)
    kernel = kernel / kernel.sum(axis=1, keepdims=True)
    return np.linalg.matrix_power(kernel, SMOOTH_PASSES)


def two_tap(ids, first, weight):
    d = ids - first
    return jnp.where(d == 0, 1.0 - weight, jnp.where(d == 1, weight, 0.0)).astype(jnp.bfloat16)


def render_kernel(all_rows, sec, above, below, rshift, rfrac, cshift, cfrac, out, stack, mix):
    n_rows, n_cols = sec.shape
    tile = lax.axis_index("ty")
    stack[0:MARGIN] = above[...]
    stack[MARGIN : MARGIN + n_rows] = sec[...]
    stack[MARGIN + n_rows :] = below[...]
    span = PATCH + 2 * MARGIN
    for p in range(n_rows // PATCH):
        at = p * PATCH
        y = tile * n_rows + at + lax.broadcasted_iota(jnp.int32, (1, PATCH), 1)
        src = jnp.clip(y + rshift[:, at : at + PATCH], 0, all_rows - 2)
        src = src - (tile * n_rows - MARGIN + at)
        weight = rfrac[:, at : at + PATCH].astype(jnp.float32) / 256.0
        ids = lax.broadcasted_iota(jnp.int32, (span, PATCH), 0)
        table = two_tap(ids, src, weight)
        mix[at : at + PATCH] = lax.dot_general(
            table,
            stack[at : at + span],
            (((0,), (0,)), ((), ())),
            preferred_element_type=jnp.float32,
        ).astype(jnp.bfloat16)
    for x0 in range(0, n_cols, BLOCK):
        lo, hi = max(x0 - PATCH, 0), min(x0 + BLOCK + PATCH, n_cols)
        x = x0 + lax.broadcasted_iota(jnp.int32, (1, BLOCK), 1)
        src = jnp.clip(x + cshift[:, x0 : x0 + BLOCK], 0, n_cols - 2) - lo
        weight = cfrac[:, x0 : x0 + BLOCK].astype(jnp.float32) / 256.0
        ids = lax.broadcasted_iota(jnp.int32, (hi - lo, BLOCK), 0)
        table = two_tap(ids, src, weight)
        out[:, x0 : x0 + BLOCK] = jnp.dot(
            mix[:, lo:hi], table, preferred_element_type=jnp.float32
        ).astype(jnp.bfloat16)


def patch_sums(a, b, py, px):
    a = a.astype(jnp.float32)
    b = b.astype(jnp.float32)
    b = pltpu.roll(b, (PATCH - px) % PATCH, 1)
    b = pltpu.roll(b, (PATCH - py) % PATCH, 0)
    bs = (pltpu.roll(b, 1, 0), b, pltpu.roll(b, PATCH - 1, 0))
    sums = []
    as_ = (pltpu.roll(a, PATCH - 1, 1), a, pltpu.roll(a, 1, 1))
    for dy in range(3):
        for dx in range(3):
            sums.append(jnp.sum(as_[dx] * bs[dy], axis=0, keepdims=True))
    return sums


def flow_from(acc, peaks):
    w = [jnp.maximum(jnp.sum(acc[k], axis=-1, keepdims=True) / PATCH, 0.0) for k in range(9)]
    total = jnp.maximum(functools.reduce(lambda p, q: p + q, w), 1.0)
    row = (w[6] + w[7] + w[8]) - (w[0] + w[1] + w[2])
    col = (w[2] + w[5] + w[8]) - (w[0] + w[3] + w[6])
    return peaks[0] + row / total, peaks[1] + col / total


def window_kernel(peak, cur, shifted, boundary, out, old, acc, peaks, sem):
    n_rows, n_cols = cur.shape
    n_px = n_cols // PATCH
    first = lax.axis_index("gz") == 0

    @pl.when(first)
    def _():
        pltpu.make_async_copy(boundary, old, sem).start()

    @pl.when(jnp.logical_not(first))
    def _():
        pltpu.make_async_copy(shifted, old, sem).start()

    pltpu.make_async_copy(shifted, old, sem).wait()

    def column(j, carry):
        cols = pl.ds(pl.multiple_of(j * PATCH, PATCH), PATCH)
        for p in range(n_rows // PATCH):
            rows = slice(p * PATCH, (p + 1) * PATCH)
            py, px = peak[0, p * n_px + j], peak[1, p * n_px + j]
            sums = patch_sums(cur[rows, cols], old[rows, cols], py, px)
            at = pl.ds(p * n_px + j, 1)
            for k in range(9):
                acc[k, at, :] = sums[k]
            peaks[0, at, :] = jnp.full((1, PATCH), py, jnp.int32).astype(jnp.float32)
            peaks[1, at, :] = jnp.full((1, PATCH), px, jnp.int32).astype(jnp.float32)
        return carry

    lax.fori_loop(0, n_px, column, 0)
    row, col = flow_from(acc, peaks)
    out[0] = row
    out[1] = col


def shift(x, axis, by):
    peers = lax.axis_size(axis)
    pairs = [(i, i + by) for i in range(peers) if 0 <= i + by < peers]
    return lax.ppermute(x, axis, pairs)


def local(sections, boundary, row_shift, row_frac, col_shift, col_frac, peak_shift):
    n_rows, n_cols = sections.shape[1:]
    tile = lax.axis_index("ty")
    tiles = lax.axis_size("ty")
    sec = sections[0]
    above = shift(sec[n_rows - MARGIN :], "ty", 1)
    below = shift(sec[:MARGIN], "ty", -1)
    rendered = pl.pallas_call(
        functools.partial(render_kernel, n_rows * tiles),
        out_shape=jax.ShapeDtypeStruct((n_rows, n_cols), jnp.bfloat16),
        scratch_shapes=[
            pltpu.VMEM((n_rows + 2 * MARGIN, n_cols), jnp.bfloat16),
            pltpu.VMEM((n_rows, n_cols), jnp.bfloat16),
        ],
    )(sec, above, below, row_shift, row_frac, col_shift, col_frac)
    shifted = shift(rendered, "gz", 1)
    patch_rows, patch_cols = n_rows // PATCH, n_cols // PATCH
    n_patches = patch_rows * patch_cols
    any_spec = pl.BlockSpec(memory_space=pl.ANY)
    vmem_spec = pl.BlockSpec(memory_space=pltpu.VMEM)
    raw = pl.pallas_call(
        window_kernel,
        out_shape=jax.ShapeDtypeStruct((2, n_patches, PATCH), jnp.float32),
        in_specs=[pl.BlockSpec(memory_space=pltpu.SMEM), vmem_spec, any_spec, any_spec],
        out_specs=vmem_spec,
        scratch_shapes=[
            pltpu.VMEM((n_rows, n_cols), jnp.bfloat16),
            pltpu.VMEM((9, n_patches, PATCH), jnp.float32),
            pltpu.VMEM((2, n_patches, PATCH), jnp.float32),
            pltpu.SemaphoreType.DMA,
        ],
    )(peak_shift.reshape(2, n_patches), rendered, shifted, boundary)
    raw = raw[:, :, 0].reshape(2, patch_rows, patch_cols)
    reach = 2 * SMOOTH_PASSES
    hops = -(-reach // patch_rows)
    parts = [shift(raw, "ty", h) if h else raw for h in range(hops, -hops - 1, -1)]
    field = jnp.concatenate(parts, axis=1)
    width = field.shape[1]
    pad = hops * patch_rows
    rows_op = np.pad(smooth_operator(patch_rows * tiles), ((0, 0), (pad, pad))).astype(np.float32)
    at = tile * patch_rows
    rows_op = lax.dynamic_slice(jnp.asarray(rows_op), (at, at), (patch_rows, width))
    cols_op = jnp.asarray(smooth_operator(patch_cols).astype(np.float32))
    flow = jnp.einsum("yr,crx->cyx", rows_op, field, precision=lax.Precision.HIGHEST)
    flow = jnp.einsum("cyr,xr->cyx", flow, cols_op, precision=lax.Precision.HIGHEST)
    return rendered[None], flow[:, None]


def solution(mesh):
    in_specs = (
        P(("parts", "gz"), "ty", None),
        P(("parts", "ty"), None),
        P(("parts", "gz"), "ty"),
        P(("parts", "gz"), "ty"),
        P(("parts", "gz"), None),
        P(("parts", "gz"), None),
        P(None, ("parts", "gz"), "ty", None),
    )
    out_specs = (P(("parts", "gz"), "ty", None), P(None, ("parts", "gz"), "ty", None))
    return jax.shard_map(local, mesh=mesh, in_specs=in_specs, out_specs=out_specs, check_vma=False)
```

```python
import functools

import jax
import jax.numpy as jnp
import numpy as np
from jax import lax
from jax.experimental import pallas as pl
from jax.experimental.pallas import tpu as pltpu
from jax.sharding import PartitionSpec as P

PATCH = 128
MARGIN = 64
SMOOTH_PASSES = 2
TAPS = (0.0625, 0.25, 0.375, 0.25, 0.0625)
BLOCK = 256
CHUNK = 512
WRAP = 16
MESH = pl.DeviceIdType.MESH


def smooth_operator(n):
    kernel = np.zeros((n, n))
    for k, tap in enumerate(TAPS):
        kernel += tap * np.eye(n, k=k - 2)
    kernel = kernel / kernel.sum(axis=1, keepdims=True)
    return np.linalg.matrix_power(kernel, SMOOTH_PASSES)


def tile_operators(tiles, patch_rows, patch_cols, hops):
    pad = hops * patch_rows
    rows = np.pad(smooth_operator(tiles * patch_rows), ((0, 0), (pad, pad)))
    cols = smooth_operator(patch_cols)
    ops = []
    for tile in range(tiles):
        at = tile * patch_rows
        ops.append(np.kron(rows[at : at + patch_rows, at : at + patch_rows + 2 * pad], cols))
    return np.stack(ops).astype(np.float32)


def two_tap(ids, first, weight):
    d = ids - first
    return jnp.where(d == 0, 1.0 - weight, jnp.where(d == 1, weight, 0.0)).astype(jnp.bfloat16)


def kernel(
    hops,
    sec, boundary, rshift, rfrac, cshift, cfrac, peak, ops,
    rendered, flow,
    stack, tabs, mix, cur, old, bpad, acc, peaks, field, op,
    local_sem, halo_send, halo_recv, mid_send, mid_recv, edge_send, edge_recv, flow_send, flow_recv,
):
    n_rows, n_cols = sec.shape[1:]
    n_px = n_cols // PATCH
    patch_rows = n_rows // PATCH
    chunks = n_cols // CHUNK
    tile, gz = lax.axis_index("ty"), lax.axis_index("gz")
    tiles, sections = lax.axis_size("ty"), lax.axis_size("gz")
    all_rows = n_rows * tiles

    def ty_ok(h):
        return jnp.logical_and(tile + h >= 0, tile + h < tiles)

    has_next, has_prev = gz + 1 < sections, gz > 0
    first = gz == 0
    ty_hops = [h for h in range(-hops, hops + 1) if h]
    peers = [({"ty": tile + h}, ty_ok(h)) for h in ty_hops]
    peers += [({"gz": gz + 1}, has_next), ({"gz": gz - 1}, has_prev)]

    load_sec = pltpu.make_async_copy(
        sec.at[0], stack.at[pl.ds(MARGIN, n_rows)], local_sem.at[0]
    )
    load_sec.start()
    load_op = pltpu.make_async_copy(ops.at[tile], op, local_sem.at[1])
    load_op.start()
    load_old = pltpu.make_async_copy(boundary, old, local_sem.at[2])

    @pl.when(first)
    def _():
        load_old.start()

    barrier = pltpu.get_barrier_semaphore()
    for where, ok in peers:
        @pl.when(ok)
        def _(where=where):
            pl.semaphore_signal(barrier, inc=1, device_id=where, device_id_type=MESH)
    pl.semaphore_wait(barrier, sum(jnp.where(ok, 1, 0) for _, ok in peers))

    down = pltpu.make_async_remote_copy(
        src_ref=sec.at[0, pl.ds(n_rows - MARGIN, MARGIN)],
        dst_ref=stack.at[pl.ds(0, MARGIN)],
        send_sem=halo_send.at[0], recv_sem=halo_recv.at[0],
        device_id={"ty": tile + 1}, device_id_type=MESH,
    )
    up = pltpu.make_async_remote_copy(
        src_ref=sec.at[0, pl.ds(0, MARGIN)],
        dst_ref=stack.at[pl.ds(MARGIN + n_rows, MARGIN)],
        send_sem=halo_send.at[1], recv_sem=halo_recv.at[1],
        device_id={"ty": tile - 1}, device_id_type=MESH,
    )

    @pl.when(ty_ok(1))
    def _():
        down.start()

    @pl.when(ty_ok(-1))
    def _():
        up.start()

    @pl.when(jnp.logical_not(ty_ok(-1)))
    def _():
        stack[0:MARGIN] = jnp.zeros((MARGIN, n_cols), jnp.bfloat16)

    @pl.when(jnp.logical_not(ty_ok(1)))
    def _():
        stack[MARGIN + n_rows :] = jnp.zeros((MARGIN, n_cols), jnp.bfloat16)

    for h in ty_hops:
        @pl.when(jnp.logical_not(ty_ok(h)))
        def _(h=h):
            field[h + hops] = jnp.zeros(field.shape[1:], jnp.float32)

    spans = []
    for b, x0 in enumerate(range(0, n_cols, BLOCK)):
        lo, hi = max(x0 - PATCH, 0), min(x0 + BLOCK + PATCH, n_cols)
        spans.append((x0, lo, hi))
        x = x0 + lax.broadcasted_iota(jnp.int32, (1, BLOCK), 1)
        src = jnp.clip(x + cshift[:, x0 : x0 + BLOCK], 0, n_cols - 2) - lo
        weight = cfrac[:, x0 : x0 + BLOCK].astype(jnp.float32) / 256.0
        ids = lax.broadcasted_iota(jnp.int32, (hi - lo, BLOCK), 0)
        tabs[b, 0 : hi - lo, :] = two_tap(ids, src, weight)

    y = tile * n_rows + lax.broadcasted_iota(jnp.int32, (1, n_rows), 1)
    src_row = jnp.clip(y + rshift[...], 0, all_rows - 2) - (tile * n_rows - MARGIN)
    row_weight = rfrac[...].astype(jnp.float32) / 256.0

    def mix_rows(o0, o1):
        g0, g1 = o0 // PATCH * PATCH, -(-o1 // PATCH) * PATCH
        span = o1 - o0 + 2 * MARGIN
        ids = o0 + lax.broadcasted_iota(jnp.int32, (span, g1 - g0), 0)
        table = two_tap(ids, src_row[:, g0:g1], row_weight[:, g0:g1])
        full = lax.dot_general(
            table, stack[o0 : o0 + span], (((0,), (0,)), ((), ())),
            preferred_element_type=jnp.float32,
        )
        return full[o0 - g0 : o1 - g0].astype(jnp.bfloat16)

    load_sec.wait()
    m0, m1 = MARGIN, n_rows - MARGIN
    for at in range(m0, m1, PATCH):
        mix[at : at + PATCH] = mix_rows(at, at + PATCH)

    def next_copy(rows, cols, send, recv):
        return pltpu.make_async_remote_copy(
            src_ref=cur.at[rows, cols], dst_ref=old.at[rows, cols],
            send_sem=send, recv_sem=recv,
            device_id={"gz": gz + 1}, device_id_type=MESH,
        )

    mids, tops, bots = [], [], []
    for c in range(chunks):
        cols = pl.ds(c * CHUNK, CHUNK)
        mids.append(next_copy(pl.ds(m0, m1 - m0), cols, mid_send.at[c], mid_recv.at[c]))
        tops.append(next_copy(pl.ds(0, m0), cols, edge_send.at[0, c], edge_recv.at[0, c]))
        bots.append(next_copy(pl.ds(m1, n_rows - m1), cols, edge_send.at[1, c], edge_recv.at[1, c]))

    def start_next(copies):
        @pl.when(has_next)
        def _():
            for copy in copies:
                copy.start()

    per = CHUNK // BLOCK
    for b, (x0, lo, hi) in enumerate(spans):
        cur[m0:m1, x0 : x0 + BLOCK] = jnp.dot(
            mix[m0:m1, lo:hi], tabs[b, 0 : hi - lo, :], preferred_element_type=jnp.float32
        ).astype(jnp.bfloat16)
        if b % per == per - 1:
            start_next([mids[b // per]])

    @pl.when(ty_ok(-1))
    def _():
        down.wait_recv()

    @pl.when(ty_ok(1))
    def _():
        up.wait_recv()

    mix[0:m0] = mix_rows(0, m0)
    mix[m1:n_rows] = mix_rows(m1, n_rows)
    for b, (x0, lo, hi) in enumerate(spans):
        edges = jnp.concatenate([mix[0:m0, lo:hi], mix[m1:n_rows, lo:hi]], axis=0)
        edges = jnp.dot(
            edges, tabs[b, 0 : hi - lo, :], preferred_element_type=jnp.float32
        ).astype(jnp.bfloat16)
        cur[0:m0, x0 : x0 + BLOCK] = edges[0:m0]
        cur[m1:n_rows, x0 : x0 + BLOCK] = edges[m0:]
        if b % per == per - 1:
            start_next([tops[b // per], bots[b // per]])

    save = pltpu.make_async_copy(cur, rendered.at[0], local_sem.at[3])
    save.start()

    @pl.when(first)
    def _():
        load_old.wait()

    def column(j, carry):
        cols = pl.ds(pl.multiple_of(j * PATCH, PATCH), PATCH)
        for p in range(patch_rows):
            rows = slice(p * PATCH, (p + 1) * PATCH)
            py, px = peak[0, 0, p, j], peak[1, 0, p, j]
            b = old[rows, cols].astype(jnp.float32)
            b = pltpu.roll(b, (PATCH - px) % PATCH, 1)
            bpad[p, 0:WRAP] = b[PATCH - WRAP :]
            bpad[p, WRAP : WRAP + PATCH] = b
            bpad[p, WRAP + PATCH :] = b[:WRAP]
            sums = [None] * 9
            for r in range(0, PATCH, 16):
                a = cur[p * PATCH + r : p * PATCH + r + 16, cols].astype(jnp.float32)
                a3 = (pltpu.roll(a, PATCH - 1, 1), a, pltpu.roll(a, 1, 1))
                for dy in range(3):
                    bb = bpad[p, pl.ds(WRAP - 1 + dy + r + py, 16), :]
                    for dx in range(3):
                        t = a3[dx] * bb
                        t = t[0:8] + t[8:16]
                        k = dy * 3 + dx
                        sums[k] = t if sums[k] is None else sums[k] + t
            at = pl.ds(p * n_px + j, 1)
            for k in range(9):
                acc[k, at, :] = jnp.sum(sums[k], axis=0, keepdims=True)
            peaks[0, at, :] = jnp.full((1, PATCH), py, jnp.int32).astype(jnp.float32)
            peaks[1, at, :] = jnp.full((1, PATCH), px, jnp.int32).astype(jnp.float32)
        return carry

    for c in range(chunks):
        @pl.when(has_prev)
        def _(c=c):
            mids[c].wait_recv()
            tops[c].wait_recv()
            bots[c].wait_recv()

        lax.fori_loop(c * CHUNK // PATCH, (c + 1) * CHUNK // PATCH, column, 0)

    w = [jnp.maximum(jnp.sum(acc[k], axis=-1, keepdims=True) / PATCH, 0.0) for k in range(9)]
    total = jnp.maximum(functools.reduce(lambda p, q: p + q, w), 1.0)
    row = ((w[6] + w[7] + w[8]) - (w[0] + w[1] + w[2])) / total
    col = ((w[2] + w[5] + w[8]) - (w[0] + w[3] + w[6])) / total
    lane = lax.broadcasted_iota(jnp.int32, field.shape[1:], 1)
    field[hops] = jnp.where(
        lane == 0, peaks[0] + row, jnp.where(lane == 1, peaks[1] + col, 0.0)
    )
    flows = []
    for i, h in enumerate(ty_hops):
        flows.append(
            pltpu.make_async_remote_copy(
                src_ref=field.at[hops], dst_ref=field.at[hops - h],
                send_sem=flow_send.at[i], recv_sem=flow_recv.at[i],
                device_id={"ty": tile + h}, device_id_type=MESH,
            )
        )

        @pl.when(ty_ok(h))
        def _(i=i):
            flows[i].start()

    load_op.wait()
    for i, h in enumerate(ty_hops):
        @pl.when(ty_ok(-h))
        def _(i=i):
            flows[i].wait_recv()

    wide = field.shape[0] * field.shape[1]
    smooth = lax.dot_general(
        field[...].reshape(wide, PATCH), op[...], (((0,), (1,)), ((), ())),
        preferred_element_type=jnp.float32, precision=lax.Precision.HIGHEST,
    )
    for p in range(patch_rows):
        flow[:, 0, p, :] = smooth[0:2, p * n_px : (p + 1) * n_px]

    for i, h in enumerate(ty_hops):
        @pl.when(ty_ok(h))
        def _(i=i):
            flows[i].wait_send()

    @pl.when(ty_ok(1))
    def _():
        down.wait_send()

    @pl.when(ty_ok(-1))
    def _():
        up.wait_send()

    @pl.when(has_next)
    def _():
        for copy in mids + tops + bots:
            copy.wait_send()

    save.wait()


def local(sections, boundary, row_shift, row_frac, col_shift, col_frac, peak_shift):
    n_rows, n_cols = sections.shape[1:]
    tiles = lax.axis_size("ty")
    patch_rows, patch_cols = n_rows // PATCH, n_cols // PATCH
    n_patches = patch_rows * patch_cols
    hops = -(-2 * SMOOTH_PASSES // patch_rows)
    chunks = n_cols // CHUNK
    ops = jnp.asarray(tile_operators(tiles, patch_rows, patch_cols, hops))
    anywhere = pl.BlockSpec(memory_space=pl.ANY)
    vmem = pl.BlockSpec(memory_space=pltpu.VMEM)
    smem = pl.BlockSpec(memory_space=pltpu.SMEM)
    dma = pltpu.SemaphoreType.DMA
    return pl.pallas_call(
        functools.partial(kernel, hops),
        out_shape=(
            jax.ShapeDtypeStruct(sections.shape, jnp.bfloat16),
            jax.ShapeDtypeStruct(peak_shift.shape, jnp.float32),
        ),
        in_specs=[anywhere, anywhere, vmem, vmem, vmem, vmem, smem, anywhere],
        out_specs=(anywhere, vmem),
        scratch_shapes=[
            pltpu.VMEM((n_rows + 2 * MARGIN, n_cols), jnp.bfloat16),
            pltpu.VMEM((n_cols // BLOCK, BLOCK + 2 * PATCH, BLOCK), jnp.bfloat16),
            pltpu.VMEM((n_rows, n_cols), jnp.bfloat16),
            pltpu.VMEM((n_rows, n_cols), jnp.bfloat16),
            pltpu.VMEM((n_rows, n_cols), jnp.bfloat16),
            pltpu.VMEM((patch_rows, PATCH + 2 * WRAP, PATCH), jnp.float32),
            pltpu.VMEM((9, n_patches, PATCH), jnp.float32),
            pltpu.VMEM((2, n_patches, PATCH), jnp.float32),
            pltpu.VMEM((2 * hops + 1, n_patches, PATCH), jnp.float32),
            pltpu.VMEM(ops.shape[1:], jnp.float32),
            dma((4,)), dma((2,)), dma((2,)), dma((chunks,)), dma((chunks,)),
            dma((2, chunks)), dma((2, chunks)), dma((2 * hops,)), dma((2 * hops,)),
        ],
        compiler_params=pltpu.CompilerParams(collective_id=0, has_side_effects=True),
    )(sections, boundary, row_shift, row_frac, col_shift, col_frac, peak_shift, ops)


def solution(mesh):
    in_specs = (
        P(("parts", "gz"), "ty", None),
        P(("parts", "ty"), None),
        P(("parts", "gz"), "ty"),
        P(("parts", "gz"), "ty"),
        P(("parts", "gz"), None),
        P(("parts", "gz"), None),
        P(None, ("parts", "gz"), "ty", None),
    )
    out_specs = (P(("parts", "gz"), "ty", None), P(None, ("parts", "gz"), "ty", None))
    return jax.shard_map(local, mesh=mesh, in_specs=in_specs, out_specs=out_specs, check_vma=False)
```

```python
import functools

import jax
import jax.numpy as jnp
import numpy as np
from jax import lax
from jax.experimental import pallas as pl
from jax.experimental.pallas import tpu as pltpu
from jax.sharding import PartitionSpec as P

PATCH = 128
MARGIN = 64
SMOOTH_PASSES = 2
TAPS = (0.0625, 0.25, 0.375, 0.25, 0.0625)
BLOCK = 256
CHUNK = 512
WRAP = 16
MESH = pl.DeviceIdType.MESH


def smooth_operator(n):
    kernel = np.zeros((n, n))
    for k, tap in enumerate(TAPS):
        kernel += tap * np.eye(n, k=k - 2)
    kernel = kernel / kernel.sum(axis=1, keepdims=True)
    return np.linalg.matrix_power(kernel, SMOOTH_PASSES)


def tile_operators(tiles, patch_rows, patch_cols, hops):
    pad = hops * patch_rows
    rows = np.pad(smooth_operator(tiles * patch_rows), ((0, 0), (pad, pad)))
    cols = smooth_operator(patch_cols)
    ops = []
    for tile in range(tiles):
        at = tile * patch_rows
        ops.append(np.kron(rows[at : at + patch_rows, at : at + patch_rows + 2 * pad], cols))
    return np.stack(ops).astype(np.float32)


def two_tap(ids, first, weight):
    d = ids - first
    return jnp.where(d == 0, 1.0 - weight, jnp.where(d == 1, weight, 0.0)).astype(jnp.bfloat16)


def kernel(
    hops,
    sec, boundary, rshift, rfrac, cshift, cfrac, peak, ops,
    rendered, flow,
    stack, tabs, mix, old, bpad, acc, peaks, field, op,
    local_sem, halo_send, halo_recv, mid_send, mid_recv, edge_send, edge_recv, flow_send, flow_recv,
):
    cur = rendered.at[0]
    n_rows, n_cols = sec.shape[1:]
    n_px = n_cols // PATCH
    patch_rows = n_rows // PATCH
    chunks = n_cols // CHUNK
    tile, gz = lax.axis_index("ty"), lax.axis_index("gz")
    tiles, sections = lax.axis_size("ty"), lax.axis_size("gz")
    all_rows = n_rows * tiles

    def ty_ok(h):
        return jnp.logical_and(tile + h >= 0, tile + h < tiles)

    has_next, has_prev = gz + 1 < sections, gz > 0
    first = gz == 0
    ty_hops = [h for h in range(-hops, hops + 1) if h]
    peers = [({"ty": tile + h}, ty_ok(h)) for h in ty_hops]
    peers += [({"gz": gz + 1}, has_next), ({"gz": gz - 1}, has_prev)]

    load_sec = pltpu.make_async_copy(
        sec.at[0], stack.at[pl.ds(MARGIN, n_rows)], local_sem.at[0]
    )
    load_sec.start()
    load_op = pltpu.make_async_copy(ops.at[tile], op, local_sem.at[1])
    load_op.start()
    load_old = pltpu.make_async_copy(boundary, old, local_sem.at[2])

    @pl.when(first)
    def _():
        load_old.start()

    barrier = pltpu.get_barrier_semaphore()
    for where, ok in peers:
        @pl.when(ok)
        def _(where=where):
            pl.semaphore_signal(barrier, inc=1, device_id=where, device_id_type=MESH)
    pl.semaphore_wait(barrier, sum(jnp.where(ok, 1, 0) for _, ok in peers))

    ends = [min((c + 1) * CHUNK + PATCH, n_cols) for c in range(chunks)]
    downs, ups = [], []
    for c, (x0, x1) in enumerate(zip([0] + ends, ends)):
        cols = pl.ds(x0, x1 - x0)
        downs.append(
            pltpu.make_async_remote_copy(
                src_ref=sec.at[0, pl.ds(n_rows - MARGIN, MARGIN), cols],
                dst_ref=stack.at[pl.ds(0, MARGIN), cols],
                send_sem=halo_send.at[0, c], recv_sem=halo_recv.at[0, c],
                device_id={"ty": tile + 1}, device_id_type=MESH,
            )
        )
        ups.append(
            pltpu.make_async_remote_copy(
                src_ref=sec.at[0, pl.ds(0, MARGIN), cols],
                dst_ref=stack.at[pl.ds(MARGIN + n_rows, MARGIN), cols],
                send_sem=halo_send.at[1, c], recv_sem=halo_recv.at[1, c],
                device_id={"ty": tile - 1}, device_id_type=MESH,
            )
        )
    for c in range(chunks):
        @pl.when(ty_ok(1))
        def _(c=c):
            downs[c].start()

        @pl.when(ty_ok(-1))
        def _(c=c):
            ups[c].start()

    @pl.when(jnp.logical_not(ty_ok(-1)))
    def _():
        stack[0:MARGIN] = jnp.zeros((MARGIN, n_cols), jnp.bfloat16)

    @pl.when(jnp.logical_not(ty_ok(1)))
    def _():
        stack[MARGIN + n_rows :] = jnp.zeros((MARGIN, n_cols), jnp.bfloat16)

    for h in ty_hops:
        @pl.when(jnp.logical_not(ty_ok(h)))
        def _(h=h):
            field[h + hops] = jnp.zeros(field.shape[1:], jnp.float32)

    spans = []
    for b, x0 in enumerate(range(0, n_cols, BLOCK)):
        lo, hi = max(x0 - PATCH, 0), min(x0 + BLOCK + PATCH, n_cols)
        spans.append((x0, lo, hi))
        x = x0 + lax.broadcasted_iota(jnp.int32, (1, BLOCK), 1)
        src = jnp.clip(x + cshift[:, x0 : x0 + BLOCK], 0, n_cols - 2) - lo
        weight = cfrac[:, x0 : x0 + BLOCK].astype(jnp.float32) / 256.0
        ids = lax.broadcasted_iota(jnp.int32, (hi - lo, BLOCK), 0)
        tabs[b, 0 : hi - lo, :] = two_tap(ids, src, weight)

    y = tile * n_rows + lax.broadcasted_iota(jnp.int32, (1, n_rows), 1)
    src_row = jnp.clip(y + rshift[...], 0, all_rows - 2) - (tile * n_rows - MARGIN)
    row_weight = rfrac[...].astype(jnp.float32) / 256.0

    def row_table(o0, o1):
        g0, g1 = o0 // PATCH * PATCH, -(-o1 // PATCH) * PATCH
        span = o1 - o0 + 2 * MARGIN
        ids = o0 + lax.broadcasted_iota(jnp.int32, (span, g1 - g0), 0)
        return two_tap(ids, src_row[:, g0:g1], row_weight[:, g0:g1])

    def mix_rows(table, o0, o1, x0, x1):
        g0 = o0 // PATCH * PATCH
        full = lax.dot_general(
            table, stack[o0 : o1 + 2 * MARGIN, x0:x1], (((0,), (0,)), ((), ())),
            preferred_element_type=jnp.float32,
        )
        mix[o0:o1, x0:x1] = full[o0 - g0 : o1 - g0].astype(jnp.bfloat16)

    load_sec.wait()
    m0, m1 = MARGIN, n_rows - MARGIN
    for at in range(m0, m1, PATCH):
        mix_rows(row_table(at, at + PATCH), at, at + PATCH, 0, n_cols)

    def next_copy(rows, cols, send, recv):
        return pltpu.make_async_remote_copy(
            src_ref=cur.at[rows, cols], dst_ref=old.at[rows, cols],
            send_sem=send, recv_sem=recv,
            device_id={"gz": gz + 1}, device_id_type=MESH,
        )

    mids, tops, bots = [], [], []
    for c in range(chunks):
        cols = pl.ds(c * CHUNK, CHUNK)
        mids.append(next_copy(pl.ds(m0, m1 - m0), cols, mid_send.at[c], mid_recv.at[c]))
        tops.append(next_copy(pl.ds(0, m0), cols, edge_send.at[0, c], edge_recv.at[0, c]))
        bots.append(next_copy(pl.ds(m1, n_rows - m1), cols, edge_send.at[1, c], edge_recv.at[1, c]))

    def start_next(copies):
        @pl.when(has_next)
        def _():
            for copy in copies:
                copy.start()

    per = CHUNK // BLOCK
    for b, (x0, lo, hi) in enumerate(spans):
        cur[m0:m1, x0 : x0 + BLOCK] = jnp.dot(
            mix[m0:m1, lo:hi], tabs[b, 0 : hi - lo, :], preferred_element_type=jnp.float32
        ).astype(jnp.bfloat16)
        if b % per == per - 1:
            start_next([mids[b // per]])

    top_table, bot_table = row_table(0, m0), row_table(m1, n_rows)

    def render_edges(c):
        @pl.when(ty_ok(-1))
        def _():
            downs[c].wait_recv()

        @pl.when(ty_ok(1))
        def _():
            ups[c].wait_recv()

        x0, x1 = ([0] + ends)[c], ends[c]
        mix_rows(top_table, 0, m0, x0, x1)
        mix_rows(bot_table, m1, n_rows, x0, x1)
        for b in range(c * per, (c + 1) * per):
            x0, lo, hi = spans[b]
            edges = jnp.concatenate([mix[0:m0, lo:hi], mix[m1:n_rows, lo:hi]], axis=0)
            edges = jnp.dot(
                edges, tabs[b, 0 : hi - lo, :], preferred_element_type=jnp.float32
            ).astype(jnp.bfloat16)
            cur[0:m0, x0 : x0 + BLOCK] = edges[0:m0]
            cur[m1:n_rows, x0 : x0 + BLOCK] = edges[m0:]
        start_next([tops[c], bots[c]])

    @pl.when(first)
    def _():
        load_old.wait()

    def column(j, carry):
        cols = pl.ds(pl.multiple_of(j * PATCH, PATCH), PATCH)
        for p in range(patch_rows):
            rows = slice(p * PATCH, (p + 1) * PATCH)
            py, px = peak[0, 0, p, j], peak[1, 0, p, j]
            b = old[rows, cols].astype(jnp.float32)
            b = pltpu.roll(b, (PATCH - px) % PATCH, 1)
            bpad[p, 0:WRAP] = b[PATCH - WRAP :]
            bpad[p, WRAP : WRAP + PATCH] = b
            bpad[p, WRAP + PATCH :] = b[:WRAP]
            sums = [None] * 9
            for r in range(0, PATCH, 16):
                a = cur[p * PATCH + r : p * PATCH + r + 16, cols].astype(jnp.float32)
                a3 = (pltpu.roll(a, PATCH - 1, 1), a, pltpu.roll(a, 1, 1))
                for dy in range(3):
                    bb = bpad[p, pl.ds(WRAP - 1 + dy + r + py, 16), :]
                    for dx in range(3):
                        t = a3[dx] * bb
                        t = t[0:8] + t[8:16]
                        k = dy * 3 + dx
                        sums[k] = t if sums[k] is None else sums[k] + t
            at = pl.ds(p * n_px + j, 1)
            for k in range(9):
                acc[k, at, :] = jnp.sum(sums[k], axis=0, keepdims=True)
            peaks[0, at, :] = jnp.full((1, PATCH), py, jnp.int32).astype(jnp.float32)
            peaks[1, at, :] = jnp.full((1, PATCH), px, jnp.int32).astype(jnp.float32)
        return carry

    for step in range(chunks + 1):
        if step < chunks:
            render_edges(step)
        c = step - 1
        if c < 0:
            continue

        @pl.when(has_prev)
        def _(c=c):
            mids[c].wait_recv()
            tops[c].wait_recv()
            bots[c].wait_recv()

        lax.fori_loop(c * CHUNK // PATCH, (c + 1) * CHUNK // PATCH, column, 0)

    w = [jnp.maximum(jnp.sum(acc[k], axis=-1, keepdims=True) / PATCH, 0.0) for k in range(9)]
    total = jnp.maximum(functools.reduce(lambda p, q: p + q, w), 1.0)
    row = ((w[6] + w[7] + w[8]) - (w[0] + w[1] + w[2])) / total
    col = ((w[2] + w[5] + w[8]) - (w[0] + w[3] + w[6])) / total
    lane = lax.broadcasted_iota(jnp.int32, field.shape[1:], 1)
    field[hops] = jnp.where(
        lane == 0, peaks[0] + row, jnp.where(lane == 1, peaks[1] + col, 0.0)
    )
    flows = []
    for i, h in enumerate(ty_hops):
        flows.append(
            pltpu.make_async_remote_copy(
                src_ref=field.at[hops], dst_ref=field.at[hops - h],
                send_sem=flow_send.at[i], recv_sem=flow_recv.at[i],
                device_id={"ty": tile + h}, device_id_type=MESH,
            )
        )

        @pl.when(ty_ok(h))
        def _(i=i):
            flows[i].start()

    load_op.wait()
    for i, h in enumerate(ty_hops):
        @pl.when(ty_ok(-h))
        def _(i=i):
            flows[i].wait_recv()

    wide = field.shape[0] * field.shape[1]
    smooth = lax.dot_general(
        field[...].reshape(wide, PATCH), op[...], (((0,), (1,)), ((), ())),
        preferred_element_type=jnp.float32, precision=lax.Precision.HIGHEST,
    )
    for p in range(patch_rows):
        flow[:, 0, p, :] = smooth[0:2, p * n_px : (p + 1) * n_px]

    for i, h in enumerate(ty_hops):
        @pl.when(ty_ok(h))
        def _(i=i):
            flows[i].wait_send()

    @pl.when(ty_ok(1))
    def _():
        for copy in downs:
            copy.wait_send()

    @pl.when(ty_ok(-1))
    def _():
        for copy in ups:
            copy.wait_send()

    @pl.when(has_next)
    def _():
        for copy in mids + tops + bots:
            copy.wait_send()


def local(sections, boundary, row_shift, row_frac, col_shift, col_frac, peak_shift):
    n_rows, n_cols = sections.shape[1:]
    tiles = lax.axis_size("ty")
    patch_rows, patch_cols = n_rows // PATCH, n_cols // PATCH
    n_patches = patch_rows * patch_cols
    hops = -(-2 * SMOOTH_PASSES // patch_rows)
    chunks = n_cols // CHUNK
    ops = jnp.asarray(tile_operators(tiles, patch_rows, patch_cols, hops))
    anywhere = pl.BlockSpec(memory_space=pl.ANY)
    vmem = pl.BlockSpec(memory_space=pltpu.VMEM)
    smem = pl.BlockSpec(memory_space=pltpu.SMEM)
    dma = pltpu.SemaphoreType.DMA
    return pl.pallas_call(
        functools.partial(kernel, hops),
        out_shape=(
            pltpu.VMEM(sections.shape, jnp.bfloat16),
            pltpu.VMEM(peak_shift.shape, jnp.float32),
        ),
        in_specs=[anywhere, anywhere, vmem, vmem, vmem, vmem, smem, anywhere],
        out_specs=(vmem, vmem),
        scratch_shapes=[
            pltpu.VMEM((n_rows + 2 * MARGIN, n_cols), jnp.bfloat16),
            pltpu.VMEM((n_cols // BLOCK, BLOCK + 2 * PATCH, BLOCK), jnp.bfloat16),
            pltpu.VMEM((n_rows, n_cols), jnp.bfloat16),
            pltpu.VMEM((n_rows, n_cols), jnp.bfloat16),
            pltpu.VMEM((patch_rows, PATCH + 2 * WRAP, PATCH), jnp.float32),
            pltpu.VMEM((9, n_patches, PATCH), jnp.float32),
            pltpu.VMEM((2, n_patches, PATCH), jnp.float32),
            pltpu.VMEM((2 * hops + 1, n_patches, PATCH), jnp.float32),
            pltpu.VMEM(ops.shape[1:], jnp.float32),
            dma((3,)), dma((2, chunks)), dma((2, chunks)), dma((chunks,)), dma((chunks,)),
            dma((2, chunks)), dma((2, chunks)), dma((2 * hops,)), dma((2 * hops,)),
        ],
        compiler_params=pltpu.CompilerParams(collective_id=0, has_side_effects=True),
    )(sections, boundary, row_shift, row_frac, col_shift, col_frac, peak_shift, ops)


def solution(mesh):
    in_specs = (
        P(("parts", "gz"), "ty", None),
        P(("parts", "ty"), None),
        P(("parts", "gz"), "ty"),
        P(("parts", "gz"), "ty"),
        P(("parts", "gz"), None),
        P(("parts", "gz"), None),
        P(None, ("parts", "gz"), "ty", None),
    )
    out_specs = (P(("parts", "gz"), "ty", None), P(None, ("parts", "gz"), "ty", None))
    return jax.shard_map(local, mesh=mesh, in_specs=in_specs, out_specs=out_specs, check_vma=False)
```

```python
import functools

import jax
import jax.numpy as jnp
import numpy as np
from jax import lax
from jax.experimental import pallas as pl
from jax.experimental.pallas import tpu as pltpu
from jax.sharding import PartitionSpec as P

PATCH = 128
MARGIN = 64
SMOOTH_PASSES = 2
TAPS = (0.0625, 0.25, 0.375, 0.25, 0.0625)
BLOCK = 256
CHUNK = 512
WRAP = 16
MESH = pl.DeviceIdType.MESH


def smooth_operator(n):
    kernel = np.zeros((n, n))
    for k, tap in enumerate(TAPS):
        kernel += tap * np.eye(n, k=k - 2)
    kernel = kernel / kernel.sum(axis=1, keepdims=True)
    return np.linalg.matrix_power(kernel, SMOOTH_PASSES)


def tile_operators(tiles, patch_rows, patch_cols, hops):
    pad = hops * patch_rows
    rows = np.pad(smooth_operator(tiles * patch_rows), ((0, 0), (pad, pad)))
    cols = smooth_operator(patch_cols)
    ops = []
    for tile in range(tiles):
        at = tile * patch_rows
        ops.append(np.kron(rows[at : at + patch_rows, at : at + patch_rows + 2 * pad], cols))
    return np.stack(ops).astype(np.float32)


def two_tap(ids, first, weight):
    d = ids - first
    return jnp.where(d == 0, 1.0 - weight, jnp.where(d == 1, weight, 0.0)).astype(jnp.bfloat16)


def kernel(
    hops,
    sec, boundary, rshift, rfrac, cshift, cfrac, peak, ops,
    rendered, flow,
    stack, tabs, mix, old, bpad, acc, peaks, field, op,
    local_sem, halo_send, halo_recv, mid_send, mid_recv, edge_send, edge_recv, flow_send, flow_recv,
):
    cur = rendered.at[0]
    n_rows, n_cols = sec.shape[1:]
    n_px = n_cols // PATCH
    patch_rows = n_rows // PATCH
    chunks = n_cols // CHUNK
    tile, gz = lax.axis_index("ty"), lax.axis_index("gz")
    tiles, sections = lax.axis_size("ty"), lax.axis_size("gz")
    all_rows = n_rows * tiles

    def ty_ok(h):
        return jnp.logical_and(tile + h >= 0, tile + h < tiles)

    has_next, has_prev = gz + 1 < sections, gz > 0
    first = gz == 0
    ty_hops = [h for h in range(-hops, hops + 1) if h]
    peers = [({"ty": tile + h}, ty_ok(h)) for h in ty_hops]
    peers += [({"gz": gz + 1}, has_next), ({"gz": gz - 1}, has_prev)]

    load_sec = pltpu.make_async_copy(
        sec.at[0], stack.at[pl.ds(MARGIN, n_rows)], local_sem.at[0]
    )
    load_sec.start()
    load_op = pltpu.make_async_copy(ops.at[tile], op, local_sem.at[1])
    load_op.start()
    load_old = pltpu.make_async_copy(boundary, old, local_sem.at[2])

    @pl.when(first)
    def _():
        load_old.start()

    barrier = pltpu.get_barrier_semaphore()
    for where, ok in peers:
        @pl.when(ok)
        def _(where=where):
            pl.semaphore_signal(barrier, inc=1, device_id=where, device_id_type=MESH)
    spans = []
    for x0 in range(0, n_cols, BLOCK):
        spans.append((x0, max(x0 - PATCH, 0), min(x0 + BLOCK + PATCH, n_cols)))

    def col_table(b):
        x0, lo, hi = spans[b]
        x = x0 + lax.broadcasted_iota(jnp.int32, (1, BLOCK), 1)
        src = jnp.clip(x + cshift[:, x0 : x0 + BLOCK], 0, n_cols - 2) - lo
        weight = cfrac[:, x0 : x0 + BLOCK].astype(jnp.float32) / 256.0
        ids = lax.broadcasted_iota(jnp.int32, (hi - lo, BLOCK), 0)
        tabs[b, 0 : hi - lo, :] = two_tap(ids, src, weight)

    per = CHUNK // BLOCK
    for b in range(2 * per):
        col_table(b)

    y = tile * n_rows + lax.broadcasted_iota(jnp.int32, (1, n_rows), 1)
    src_row = jnp.clip(y + rshift[...], 0, all_rows - 2) - (tile * n_rows - MARGIN)
    row_weight = rfrac[...].astype(jnp.float32) / 256.0

    pl.semaphore_wait(barrier, sum(jnp.where(ok, 1, 0) for _, ok in peers))

    ends = [min((c + 1) * CHUNK + PATCH, n_cols) for c in range(chunks)]
    downs, ups = [], []
    for c, (x0, x1) in enumerate(zip([0] + ends, ends)):
        cols = pl.ds(x0, x1 - x0)
        downs.append(
            pltpu.make_async_remote_copy(
                src_ref=sec.at[0, pl.ds(n_rows - MARGIN, MARGIN), cols],
                dst_ref=stack.at[pl.ds(0, MARGIN), cols],
                send_sem=halo_send.at[0, c], recv_sem=halo_recv.at[0, c],
                device_id={"ty": tile + 1}, device_id_type=MESH,
            )
        )
        ups.append(
            pltpu.make_async_remote_copy(
                src_ref=sec.at[0, pl.ds(0, MARGIN), cols],
                dst_ref=stack.at[pl.ds(MARGIN + n_rows, MARGIN), cols],
                send_sem=halo_send.at[1, c], recv_sem=halo_recv.at[1, c],
                device_id={"ty": tile - 1}, device_id_type=MESH,
            )
        )
    for c in range(chunks):
        @pl.when(ty_ok(1))
        def _(c=c):
            downs[c].start()

        @pl.when(ty_ok(-1))
        def _(c=c):
            ups[c].start()

    @pl.when(jnp.logical_not(ty_ok(-1)))
    def _():
        stack[0:MARGIN] = jnp.zeros((MARGIN, n_cols), jnp.bfloat16)

    @pl.when(jnp.logical_not(ty_ok(1)))
    def _():
        stack[MARGIN + n_rows :] = jnp.zeros((MARGIN, n_cols), jnp.bfloat16)

    for h in ty_hops:
        @pl.when(jnp.logical_not(ty_ok(h)))
        def _(h=h):
            field[h + hops] = jnp.zeros(field.shape[1:], jnp.float32)

    def row_table(o0, o1):
        g0, g1 = o0 // PATCH * PATCH, -(-o1 // PATCH) * PATCH
        span = o1 - o0 + 2 * MARGIN
        ids = o0 + lax.broadcasted_iota(jnp.int32, (span, g1 - g0), 0)
        return two_tap(ids, src_row[:, g0:g1], row_weight[:, g0:g1])

    def mix_rows(table, o0, o1, x0, x1):
        g0 = o0 // PATCH * PATCH
        full = lax.dot_general(
            table, stack[o0 : o1 + 2 * MARGIN, x0:x1], (((0,), (0,)), ((), ())),
            preferred_element_type=jnp.float32,
        )
        mix[o0:o1, x0:x1] = full[o0 - g0 : o1 - g0].astype(jnp.bfloat16)

    load_sec.wait()
    m0, m1 = MARGIN, n_rows - MARGIN
    mid_tables = [(at, row_table(at, at + PATCH)) for at in range(m0, m1, PATCH)]

    def next_copy(rows, cols, send, recv):
        return pltpu.make_async_remote_copy(
            src_ref=cur.at[rows, cols], dst_ref=old.at[rows, cols],
            send_sem=send, recv_sem=recv,
            device_id={"gz": gz + 1}, device_id_type=MESH,
        )

    mids, tops, bots = [], [], []
    for c in range(chunks):
        cols = pl.ds(c * CHUNK, CHUNK)
        mids.append(next_copy(pl.ds(m0, m1 - m0), cols, mid_send.at[c], mid_recv.at[c]))
        tops.append(next_copy(pl.ds(0, m0), cols, edge_send.at[0, c], edge_recv.at[0, c]))
        bots.append(next_copy(pl.ds(m1, n_rows - m1), cols, edge_send.at[1, c], edge_recv.at[1, c]))

    def start_next(copies):
        @pl.when(has_next)
        def _():
            for copy in copies:
                copy.start()

    for c in range(chunks):
        x0, x1 = ([0] + ends)[c], ends[c]
        for at, table in mid_tables:
            mix_rows(table, at, at + PATCH, x0, x1)
        for b in range(c * per, (c + 1) * per):
            if b >= 2 * per:
                col_table(b)
            x0, lo, hi = spans[b]
            cur[m0:m1, x0 : x0 + BLOCK] = jnp.dot(
                mix[m0:m1, lo:hi], tabs[b, 0 : hi - lo, :], preferred_element_type=jnp.float32
            ).astype(jnp.bfloat16)
        start_next([mids[c]])

    top_table, bot_table = row_table(0, m0), row_table(m1, n_rows)

    def render_edges(c):
        @pl.when(ty_ok(-1))
        def _():
            downs[c].wait_recv()

        @pl.when(ty_ok(1))
        def _():
            ups[c].wait_recv()

        x0, x1 = ([0] + ends)[c], ends[c]
        mix_rows(top_table, 0, m0, x0, x1)
        mix_rows(bot_table, m1, n_rows, x0, x1)
        for b in range(c * per, (c + 1) * per):
            x0, lo, hi = spans[b]
            edges = jnp.concatenate([mix[0:m0, lo:hi], mix[m1:n_rows, lo:hi]], axis=0)
            edges = jnp.dot(
                edges, tabs[b, 0 : hi - lo, :], preferred_element_type=jnp.float32
            ).astype(jnp.bfloat16)
            cur[0:m0, x0 : x0 + BLOCK] = edges[0:m0]
            cur[m1:n_rows, x0 : x0 + BLOCK] = edges[m0:]
        start_next([tops[c], bots[c]])

    @pl.when(first)
    def _():
        load_old.wait()

    def column(j, carry):
        cols = pl.ds(pl.multiple_of(j * PATCH, PATCH), PATCH)
        for p in range(patch_rows):
            rows = slice(p * PATCH, (p + 1) * PATCH)
            py, px = peak[0, 0, p, j], peak[1, 0, p, j]
            b = old[rows, cols].astype(jnp.float32)
            b = pltpu.roll(b, (PATCH - px) % PATCH, 1)
            bpad[p, 0:WRAP] = b[PATCH - WRAP :]
            bpad[p, WRAP : WRAP + PATCH] = b
            bpad[p, WRAP + PATCH :] = b[:WRAP]
            sums = [None] * 9
            for r in range(0, PATCH, 16):
                a = cur[p * PATCH + r : p * PATCH + r + 16, cols].astype(jnp.float32)
                a3 = (pltpu.roll(a, PATCH - 1, 1), a, pltpu.roll(a, 1, 1))
                for dy in range(3):
                    bb = bpad[p, pl.ds(WRAP - 1 + dy + r + py, 16), :]
                    for dx in range(3):
                        t = a3[dx] * bb
                        t = t[0:8] + t[8:16]
                        k = dy * 3 + dx
                        sums[k] = t if sums[k] is None else sums[k] + t
            at = pl.ds(p * n_px + j, 1)
            for k in range(9):
                acc[k, at, :] = jnp.sum(sums[k], axis=0, keepdims=True)
            peaks[0, at, :] = jnp.full((1, PATCH), py, jnp.int32).astype(jnp.float32)
            peaks[1, at, :] = jnp.full((1, PATCH), px, jnp.int32).astype(jnp.float32)
        return carry

    for step in range(chunks + 1):
        if step < chunks:
            render_edges(step)
        c = step - 1
        if c < 0:
            continue

        @pl.when(has_prev)
        def _(c=c):
            mids[c].wait_recv()
            tops[c].wait_recv()
            bots[c].wait_recv()

        lax.fori_loop(c * CHUNK // PATCH, (c + 1) * CHUNK // PATCH, column, 0)

    w = [jnp.maximum(jnp.sum(acc[k], axis=-1, keepdims=True) / PATCH, 0.0) for k in range(9)]
    total = jnp.maximum(functools.reduce(lambda p, q: p + q, w), 1.0)
    row = ((w[6] + w[7] + w[8]) - (w[0] + w[1] + w[2])) / total
    col = ((w[2] + w[5] + w[8]) - (w[0] + w[3] + w[6])) / total
    lane = lax.broadcasted_iota(jnp.int32, field.shape[1:], 1)
    field[hops] = jnp.where(
        lane == 0, peaks[0] + row, jnp.where(lane == 1, peaks[1] + col, 0.0)
    )
    flows = []
    for i, h in enumerate(ty_hops):
        flows.append(
            pltpu.make_async_remote_copy(
                src_ref=field.at[hops], dst_ref=field.at[hops - h],
                send_sem=flow_send.at[i], recv_sem=flow_recv.at[i],
                device_id={"ty": tile + h}, device_id_type=MESH,
            )
        )

        @pl.when(ty_ok(h))
        def _(i=i):
            flows[i].start()

    load_op.wait()
    for i, h in enumerate(ty_hops):
        @pl.when(ty_ok(-h))
        def _(i=i):
            flows[i].wait_recv()

    wide = field.shape[0] * field.shape[1]
    smooth = lax.dot_general(
        field[...].reshape(wide, PATCH), op[...], (((0,), (1,)), ((), ())),
        preferred_element_type=jnp.float32, precision=lax.Precision.HIGHEST,
    )
    for p in range(patch_rows):
        flow[:, 0, p, :] = smooth[0:2, p * n_px : (p + 1) * n_px]

    for i, h in enumerate(ty_hops):
        @pl.when(ty_ok(h))
        def _(i=i):
            flows[i].wait_send()

    @pl.when(ty_ok(1))
    def _():
        for copy in downs:
            copy.wait_send()

    @pl.when(ty_ok(-1))
    def _():
        for copy in ups:
            copy.wait_send()

    @pl.when(has_next)
    def _():
        for copy in mids + tops + bots:
            copy.wait_send()


def write_kernel(a, b, out_a, out_b, sem):
    copies = [pltpu.make_async_copy(a, out_a, sem.at[0]), pltpu.make_async_copy(b, out_b, sem.at[1])]
    for copy in copies:
        copy.start()
    for copy in copies:
        copy.wait()


def local(sections, boundary, row_shift, row_frac, col_shift, col_frac, peak_shift):
    n_rows, n_cols = sections.shape[1:]
    tiles = lax.axis_size("ty")
    patch_rows, patch_cols = n_rows // PATCH, n_cols // PATCH
    n_patches = patch_rows * patch_cols
    hops = -(-2 * SMOOTH_PASSES // patch_rows)
    chunks = n_cols // CHUNK
    ops = jnp.asarray(tile_operators(tiles, patch_rows, patch_cols, hops))
    anywhere = pl.BlockSpec(memory_space=pl.ANY)
    vmem = pl.BlockSpec(memory_space=pltpu.VMEM)
    smem = pl.BlockSpec(memory_space=pltpu.SMEM)
    dma = pltpu.SemaphoreType.DMA
    held = pl.pallas_call(
        functools.partial(kernel, hops),
        out_shape=(
            pltpu.VMEM(sections.shape, jnp.bfloat16),
            pltpu.VMEM(peak_shift.shape, jnp.float32),
        ),
        in_specs=[anywhere, anywhere, vmem, vmem, vmem, vmem, smem, anywhere],
        out_specs=(vmem, vmem),
        scratch_shapes=[
            pltpu.VMEM((n_rows + 2 * MARGIN, n_cols), jnp.bfloat16),
            pltpu.VMEM((n_cols // BLOCK, BLOCK + 2 * PATCH, BLOCK), jnp.bfloat16),
            pltpu.VMEM((n_rows, n_cols), jnp.bfloat16),
            pltpu.VMEM((n_rows, n_cols), jnp.bfloat16),
            pltpu.VMEM((patch_rows, PATCH + 2 * WRAP, PATCH), jnp.float32),
            pltpu.VMEM((9, n_patches, PATCH), jnp.float32),
            pltpu.VMEM((2, n_patches, PATCH), jnp.float32),
            pltpu.VMEM((2 * hops + 1, n_patches, PATCH), jnp.float32),
            pltpu.VMEM(ops.shape[1:], jnp.float32),
            dma((3,)), dma((2, chunks)), dma((2, chunks)), dma((chunks,)), dma((chunks,)),
            dma((2, chunks)), dma((2, chunks)), dma((2 * hops,)), dma((2 * hops,)),
        ],
        compiler_params=pltpu.CompilerParams(collective_id=0, has_side_effects=True),
    )(sections, boundary, row_shift, row_frac, col_shift, col_frac, peak_shift, ops)
    return pl.pallas_call(
        write_kernel,
        out_shape=(
            jax.ShapeDtypeStruct(sections.shape, jnp.bfloat16),
            jax.ShapeDtypeStruct(peak_shift.shape, jnp.float32),
        ),
        in_specs=[vmem, vmem],
        out_specs=(anywhere, anywhere),
        scratch_shapes=[dma((2,))],
    )(*[pltpu.with_memory_space_constraint(x, pltpu.VMEM) for x in held])


def solution(mesh):
    in_specs = (
        P(("parts", "gz"), "ty", None),
        P(("parts", "ty"), None),
        P(("parts", "gz"), "ty"),
        P(("parts", "gz"), "ty"),
        P(("parts", "gz"), None),
        P(("parts", "gz"), None),
        P(None, ("parts", "gz"), "ty", None),
    )
    out_specs = (P(("parts", "gz"), "ty", None), P(None, ("parts", "gz"), "ty", None))
    return jax.shard_map(local, mesh=mesh, in_specs=in_specs, out_specs=out_specs, check_vma=False)
```

```python
import functools

import jax
import jax.numpy as jnp
import numpy as np
from jax import lax
from jax.experimental import pallas as pl
from jax.experimental.pallas import tpu as pltpu
from jax.sharding import PartitionSpec as P

PATCH = 128
MARGIN = 64
SMOOTH_PASSES = 2
TAPS = (0.0625, 0.25, 0.375, 0.25, 0.0625)
BLOCK = 256
CHUNK = 256
EARLY = 4
WRAP = 16
MESH = pl.DeviceIdType.MESH


def smooth_operator(n):
    kernel = np.zeros((n, n))
    for k, tap in enumerate(TAPS):
        kernel += tap * np.eye(n, k=k - 2)
    kernel = kernel / kernel.sum(axis=1, keepdims=True)
    return np.linalg.matrix_power(kernel, SMOOTH_PASSES)


def tile_operators(tiles, patch_rows, patch_cols, hops):
    pad = hops * patch_rows
    rows = np.pad(smooth_operator(tiles * patch_rows), ((0, 0), (pad, pad)))
    cols = smooth_operator(patch_cols)
    ops = []
    for tile in range(tiles):
        at = tile * patch_rows
        ops.append(np.kron(rows[at : at + patch_rows, at : at + patch_rows + 2 * pad], cols))
    return np.stack(ops).astype(np.float32)


def two_tap(ids, first, weight):
    d = ids - first
    return jnp.where(d == 0, 1.0 - weight, jnp.where(d == 1, weight, 0.0)).astype(jnp.bfloat16)


def kernel(
    hops,
    sec, boundary, rshift, rfrac, cshift, cfrac, peak, ops,
    rendered, flow,
    stack, tabs, mix, old, bpad, acc, peaks, field, op,
    local_sem, halo_send, halo_recv, mid_send, mid_recv, edge_send, edge_recv, flow_send, flow_recv,
):
    cur = rendered.at[0]
    n_rows, n_cols = sec.shape[1:]
    n_px = n_cols // PATCH
    patch_rows = n_rows // PATCH
    chunks = n_cols // CHUNK
    tile, gz = lax.axis_index("ty"), lax.axis_index("gz")
    tiles, sections = lax.axis_size("ty"), lax.axis_size("gz")
    all_rows = n_rows * tiles

    def ty_ok(h):
        return jnp.logical_and(tile + h >= 0, tile + h < tiles)

    has_next, has_prev = gz + 1 < sections, gz > 0
    first = gz == 0
    ty_hops = [h for h in range(-hops, hops + 1) if h]
    peers = [({"ty": tile + h}, ty_ok(h)) for h in ty_hops if abs(h) != 2]
    peers += [({"gz": gz + 1}, has_next), ({"gz": gz - 1}, has_prev)]

    load_sec = pltpu.make_async_copy(
        sec.at[0], stack.at[pl.ds(MARGIN, n_rows)], local_sem.at[0]
    )
    load_sec.start()
    load_op = pltpu.make_async_copy(ops.at[tile], op, local_sem.at[1])
    load_op.start()
    load_old = pltpu.make_async_copy(boundary, old, local_sem.at[2])

    @pl.when(first)
    def _():
        load_old.start()

    barrier = pltpu.get_barrier_semaphore()
    for where, ok in peers:
        @pl.when(ok)
        def _(where=where):
            pl.semaphore_signal(barrier, inc=1, device_id=where, device_id_type=MESH)
    spans = []
    for x0 in range(0, n_cols, BLOCK):
        spans.append((x0, max(x0 - PATCH, 0), min(x0 + BLOCK + PATCH, n_cols)))

    def col_table(b):
        x0, lo, hi = spans[b]
        x = x0 + lax.broadcasted_iota(jnp.int32, (1, BLOCK), 1)
        src = jnp.clip(x + cshift[:, x0 : x0 + BLOCK], 0, n_cols - 2) - lo
        weight = cfrac[:, x0 : x0 + BLOCK].astype(jnp.float32) / 256.0
        ids = lax.broadcasted_iota(jnp.int32, (hi - lo, BLOCK), 0)
        tabs[b, 0 : hi - lo, :] = two_tap(ids, src, weight)

    per = CHUNK // BLOCK
    for b in range(min(EARLY, len(spans))):
        col_table(b)

    y = tile * n_rows + lax.broadcasted_iota(jnp.int32, (1, n_rows), 1)
    src_row = jnp.clip(y + rshift[...], 0, all_rows - 2) - (tile * n_rows - MARGIN)
    row_weight = rfrac[...].astype(jnp.float32) / 256.0

    pl.semaphore_wait(barrier, sum(jnp.where(ok, 1, 0) for _, ok in peers))

    ends = [min((c + 1) * CHUNK + PATCH, n_cols) for c in range(chunks)]
    downs, ups = [], []
    for c, (x0, x1) in enumerate(zip([0] + ends, ends)):
        cols = pl.ds(x0, x1 - x0)
        downs.append(
            pltpu.make_async_remote_copy(
                src_ref=sec.at[0, pl.ds(n_rows - MARGIN, MARGIN), cols],
                dst_ref=stack.at[pl.ds(0, MARGIN), cols],
                send_sem=halo_send.at[0, c], recv_sem=halo_recv.at[0, c],
                device_id={"ty": tile + 1}, device_id_type=MESH,
            )
        )
        ups.append(
            pltpu.make_async_remote_copy(
                src_ref=sec.at[0, pl.ds(0, MARGIN), cols],
                dst_ref=stack.at[pl.ds(MARGIN + n_rows, MARGIN), cols],
                send_sem=halo_send.at[1, c], recv_sem=halo_recv.at[1, c],
                device_id={"ty": tile - 1}, device_id_type=MESH,
            )
        )
    for c in range(chunks):
        @pl.when(ty_ok(1))
        def _(c=c):
            downs[c].start()

        @pl.when(ty_ok(-1))
        def _(c=c):
            ups[c].start()

    @pl.when(jnp.logical_not(ty_ok(-1)))
    def _():
        stack[0:MARGIN] = jnp.zeros((MARGIN, n_cols), jnp.bfloat16)

    @pl.when(jnp.logical_not(ty_ok(1)))
    def _():
        stack[MARGIN + n_rows :] = jnp.zeros((MARGIN, n_cols), jnp.bfloat16)

    for h in ty_hops:
        @pl.when(jnp.logical_not(ty_ok(h)))
        def _(h=h):
            field[h + hops] = jnp.zeros(field.shape[1:], jnp.float32)

    def row_table(o0, o1):
        g0, g1 = o0 // PATCH * PATCH, -(-o1 // PATCH) * PATCH
        span = o1 - o0 + 2 * MARGIN
        ids = o0 + lax.broadcasted_iota(jnp.int32, (span, g1 - g0), 0)
        return two_tap(ids, src_row[:, g0:g1], row_weight[:, g0:g1])

    def mix_rows(table, o0, o1, x0, x1):
        g0 = o0 // PATCH * PATCH
        full = lax.dot_general(
            table, stack[o0 : o1 + 2 * MARGIN, x0:x1], (((0,), (0,)), ((), ())),
            preferred_element_type=jnp.float32,
        )
        mix[o0:o1, x0:x1] = full[o0 - g0 : o1 - g0].astype(jnp.bfloat16)

    load_sec.wait()
    m0, m1 = MARGIN, n_rows - MARGIN
    mid_tables = [(at, row_table(at, at + PATCH)) for at in range(m0, m1, PATCH)]

    def next_copy(rows, cols, send, recv):
        return pltpu.make_async_remote_copy(
            src_ref=cur.at[rows, cols], dst_ref=old.at[rows, cols],
            send_sem=send, recv_sem=recv,
            device_id={"gz": gz + 1}, device_id_type=MESH,
        )

    mids, tops, bots = [], [], []
    for c in range(chunks):
        cols = pl.ds(c * CHUNK, CHUNK)
        mids.append(next_copy(pl.ds(m0, m1 - m0), cols, mid_send.at[c], mid_recv.at[c]))
        tops.append(next_copy(pl.ds(0, m0), cols, edge_send.at[0, c], edge_recv.at[0, c]))
        bots.append(next_copy(pl.ds(m1, n_rows - m1), cols, edge_send.at[1, c], edge_recv.at[1, c]))

    def start_next(copies):
        @pl.when(has_next)
        def _():
            for copy in copies:
                copy.start()

    for c in range(chunks):
        x0, x1 = ([0] + ends)[c], ends[c]
        for at, table in mid_tables:
            mix_rows(table, at, at + PATCH, x0, x1)
        for b in range(c * per, (c + 1) * per):
            if b >= EARLY:
                col_table(b)
            x0, lo, hi = spans[b]
            cur[m0:m1, x0 : x0 + BLOCK] = jnp.dot(
                mix[m0:m1, lo:hi], tabs[b, 0 : hi - lo, :], preferred_element_type=jnp.float32
            ).astype(jnp.bfloat16)
        start_next([mids[c]])

    top_table, bot_table = row_table(0, m0), row_table(m1, n_rows)

    def render_edges(c):
        @pl.when(ty_ok(-1))
        def _():
            downs[c].wait_recv()

        @pl.when(ty_ok(1))
        def _():
            ups[c].wait_recv()

        x0, x1 = ([0] + ends)[c], ends[c]
        mix_rows(top_table, 0, m0, x0, x1)
        mix_rows(bot_table, m1, n_rows, x0, x1)
        for b in range(c * per, (c + 1) * per):
            x0, lo, hi = spans[b]
            edges = jnp.concatenate([mix[0:m0, lo:hi], mix[m1:n_rows, lo:hi]], axis=0)
            edges = jnp.dot(
                edges, tabs[b, 0 : hi - lo, :], preferred_element_type=jnp.float32
            ).astype(jnp.bfloat16)
            cur[0:m0, x0 : x0 + BLOCK] = edges[0:m0]
            cur[m1:n_rows, x0 : x0 + BLOCK] = edges[m0:]
        start_next([tops[c], bots[c]])

    @pl.when(first)
    def _():
        load_old.wait()

    def column(j, carry):
        cols = pl.ds(pl.multiple_of(j * PATCH, PATCH), PATCH)
        for p in range(patch_rows):
            rows = slice(p * PATCH, (p + 1) * PATCH)
            py, px = peak[0, 0, p, j], peak[1, 0, p, j]
            b = old[rows, cols].astype(jnp.float32)
            b = pltpu.roll(b, (PATCH - px) % PATCH, 1)
            bpad[p, 0:WRAP] = b[PATCH - WRAP :]
            bpad[p, WRAP : WRAP + PATCH] = b
            bpad[p, WRAP + PATCH :] = b[:WRAP]
            sums = [None] * 9
            for r in range(0, PATCH, 16):
                a = cur[p * PATCH + r : p * PATCH + r + 16, cols].astype(jnp.float32)
                a3 = (pltpu.roll(a, PATCH - 1, 1), a, pltpu.roll(a, 1, 1))
                for dy in range(3):
                    bb = bpad[p, pl.ds(WRAP - 1 + dy + r + py, 16), :]
                    for dx in range(3):
                        t = a3[dx] * bb
                        t = t[0:8] + t[8:16]
                        k = dy * 3 + dx
                        sums[k] = t if sums[k] is None else sums[k] + t
            at = pl.ds(p * n_px + j, 1)
            for k in range(9):
                acc[k, at, :] = jnp.sum(sums[k], axis=0, keepdims=True)
            peaks[0, at, :] = jnp.full((1, PATCH), py, jnp.int32).astype(jnp.float32)
            peaks[1, at, :] = jnp.full((1, PATCH), px, jnp.int32).astype(jnp.float32)
        return carry

    for step in range(chunks + 1):
        if step < chunks:
            render_edges(step)
        c = step - 1
        if c < 0:
            continue

        @pl.when(has_prev)
        def _(c=c):
            mids[c].wait_recv()
            tops[c].wait_recv()
            bots[c].wait_recv()

        lax.fori_loop(c * CHUNK // PATCH, (c + 1) * CHUNK // PATCH, column, 0)

    w = [jnp.maximum(jnp.sum(acc[k], axis=-1, keepdims=True) / PATCH, 0.0) for k in range(9)]
    total = jnp.maximum(functools.reduce(lambda p, q: p + q, w), 1.0)
    row = ((w[6] + w[7] + w[8]) - (w[0] + w[1] + w[2])) / total
    col = ((w[2] + w[5] + w[8]) - (w[0] + w[3] + w[6])) / total
    lane = lax.broadcasted_iota(jnp.int32, field.shape[1:], 1)
    field[hops] = jnp.where(
        lane == 0, peaks[0] + row, jnp.where(lane == 1, peaks[1] + col, 0.0)
    )
    flows = []
    for i, h in enumerate(ty_hops):
        flows.append(
            pltpu.make_async_remote_copy(
                src_ref=field.at[hops], dst_ref=field.at[hops - h],
                send_sem=flow_send.at[i], recv_sem=flow_recv.at[i],
                device_id={"ty": tile + h}, device_id_type=MESH,
            )
        )

        @pl.when(ty_ok(h))
        def _(i=i):
            flows[i].start()

    load_op.wait()
    for i, h in enumerate(ty_hops):
        @pl.when(ty_ok(-h))
        def _(i=i):
            flows[i].wait_recv()

    wide = field.shape[0] * field.shape[1]
    smooth = lax.dot_general(
        field[...].reshape(wide, PATCH), op[...], (((0,), (1,)), ((), ())),
        preferred_element_type=jnp.float32, precision=lax.Precision.HIGHEST,
    )
    for p in range(patch_rows):
        flow[:, 0, p, :] = smooth[0:2, p * n_px : (p + 1) * n_px]

    for i, h in enumerate(ty_hops):
        @pl.when(ty_ok(h))
        def _(i=i):
            flows[i].wait_send()

    @pl.when(ty_ok(1))
    def _():
        for copy in downs:
            copy.wait_send()

    @pl.when(ty_ok(-1))
    def _():
        for copy in ups:
            copy.wait_send()

    @pl.when(has_next)
    def _():
        for copy in mids + tops + bots:
            copy.wait_send()


def write_kernel(a, b, out_a, out_b, sem):
    copies = [pltpu.make_async_copy(a, out_a, sem.at[0]), pltpu.make_async_copy(b, out_b, sem.at[1])]
    for copy in copies:
        copy.start()
    for copy in copies:
        copy.wait()


def local(sections, boundary, row_shift, row_frac, col_shift, col_frac, peak_shift):
    n_rows, n_cols = sections.shape[1:]
    tiles = lax.axis_size("ty")
    patch_rows, patch_cols = n_rows // PATCH, n_cols // PATCH
    n_patches = patch_rows * patch_cols
    hops = -(-2 * SMOOTH_PASSES // patch_rows)
    chunks = n_cols // CHUNK
    ops = jnp.asarray(tile_operators(tiles, patch_rows, patch_cols, hops))
    anywhere = pl.BlockSpec(memory_space=pl.ANY)
    vmem = pl.BlockSpec(memory_space=pltpu.VMEM)
    smem = pl.BlockSpec(memory_space=pltpu.SMEM)
    dma = pltpu.SemaphoreType.DMA
    held = pl.pallas_call(
        functools.partial(kernel, hops),
        out_shape=(
            pltpu.VMEM(sections.shape, jnp.bfloat16),
            pltpu.VMEM(peak_shift.shape, jnp.float32),
        ),
        in_specs=[anywhere, anywhere, vmem, vmem, vmem, vmem, smem, anywhere],
        out_specs=(vmem, vmem),
        scratch_shapes=[
            pltpu.VMEM((n_rows + 2 * MARGIN, n_cols), jnp.bfloat16),
            pltpu.VMEM((n_cols // BLOCK, BLOCK + 2 * PATCH, BLOCK), jnp.bfloat16),
            pltpu.VMEM((n_rows, n_cols), jnp.bfloat16),
            pltpu.VMEM((n_rows, n_cols), jnp.bfloat16),
            pltpu.VMEM((patch_rows, PATCH + 2 * WRAP, PATCH), jnp.float32),
            pltpu.VMEM((9, n_patches, PATCH), jnp.float32),
            pltpu.VMEM((2, n_patches, PATCH), jnp.float32),
            pltpu.VMEM((2 * hops + 1, n_patches, PATCH), jnp.float32),
            pltpu.VMEM(ops.shape[1:], jnp.float32),
            dma((3,)), dma((2, chunks)), dma((2, chunks)), dma((chunks,)), dma((chunks,)),
            dma((2, chunks)), dma((2, chunks)), dma((2 * hops,)), dma((2 * hops,)),
        ],
        compiler_params=pltpu.CompilerParams(collective_id=0, has_side_effects=True),
    )(sections, boundary, row_shift, row_frac, col_shift, col_frac, peak_shift, ops)
    return pl.pallas_call(
        write_kernel,
        out_shape=(
            jax.ShapeDtypeStruct(sections.shape, jnp.bfloat16),
            jax.ShapeDtypeStruct(peak_shift.shape, jnp.float32),
        ),
        in_specs=[vmem, vmem],
        out_specs=(anywhere, anywhere),
        scratch_shapes=[dma((2,))],
    )(*[pltpu.with_memory_space_constraint(x, pltpu.VMEM) for x in held])


def solution(mesh):
    in_specs = (
        P(("parts", "gz"), "ty", None),
        P(("parts", "ty"), None),
        P(("parts", "gz"), "ty"),
        P(("parts", "gz"), "ty"),
        P(("parts", "gz"), None),
        P(("parts", "gz"), None),
        P(None, ("parts", "gz"), "ty", None),
    )
    out_specs = (P(("parts", "gz"), "ty", None), P(None, ("parts", "gz"), "ty", None))
    return jax.shard_map(local, mesh=mesh, in_specs=in_specs, out_specs=out_specs, check_vma=False)
```
